128 devices in a mesh: group: 4 (over z_hi, core), dev: 32 (over y, z_lo, x).
Axes of the slice: x: 4, y: 4, z: 4 (z_hi: 2, z_lo: 2; z = z_hi * 2 + z_lo), core: 2. Of those that a mesh axis runs over, the one named last changes fastest.
Arguments:
- couplings: bfloat16 [128, 6, 4, 512, 512], P(('group', 'dev')), may hold values from -0.0625 to 0.0625
- history: bfloat16 [32, 65536, 256], P(None, ('group', 'dev')), may hold values from -6 to 6
- diag_inverse: bfloat16 [128, 512, 512], P(('group', 'dev')), may hold values from -0.25 to 0.25
- incident: bfloat16 [2, 65536, 256], P(None, ('group', 'dev')), may hold values from -6 to 6
- targets: int32 [128, 6], P(('group', 'dev')), may hold values from 0 to 10
- delays: int32 [128, 6], P(('group', 'dev')), may hold values from 1 to 29
- counts: int32 [128], P(('group', 'dev')), may hold values from 1 to 6, as said below
Outputs:
- currents: bfloat16 [2, 65536, 256], P(None, ('group', 'dev'))
The draws below stay inside these ranges and needn't reach their ends.
Inputs may be any that keep to these rules, and one draw needn't show every extreme that they name: `counts`: slots beyond a block's count carry matrices that are not couplings. Some block uses all 6 slots.
All inputs are finite; a program needn't handle non-finite values.
Results may differ from the reference program's by a relative error of at most 0.0048.
Values sent between devices are 32-bit elements; how exact they have to be, the bound alone decides.
A program may use at most 128 MiB of HBM per device.

```python
import jax
import jax.numpy as jnp
from jax import lax

UNK = 512
EXC = 256
HIST = 32
BAND = 4
SLOTS = 6
STEPS = 2
BLOCKS = 128
UNKNOWNS = 65536
N_GROUP = 4
N_DEV = 32


def draw_counts(key, part):
    key_base, key_heavy, key_pick = jax.random.split(key, 3)
    light_load = jax.random.randint(key_base, (BLOCKS,), 1, SLOTS // 2 + 1)
    heavy_mask = jax.random.randint(key_heavy, (BLOCKS,), 0, 8) == 0
    chosen_block = jax.random.randint(key_pick, (), 0, BLOCKS)
    full_mask = heavy_mask | (jnp.arange(BLOCKS) == chosen_block)
    return jnp.where(full_mask, SLOTS, light_load).astype(jnp.int32)


def set_ends(entries, key, low, largest):
    extent = entries.shape
    spot = [jax.random.randint(jax.random.fold_in(key, axis), (), 0, extent[axis]) for axis in range(len(extent))]
    entries = entries.at[tuple(spot)].set(low)
    longest = extent.index(max(extent))
    spot[longest] = (spot[longest] + 1) % extent[longest]
    return entries.at[tuple(spot)].set(largest)


def block_scale(rng, dims, cuts, low, largest):
    level = 1.0
    for dim, blocks in cuts:
        steps = jax.random.uniform(jax.random.fold_in(jax.random.fold_in(rng, 6), dim), (blocks,), jnp.float32, low / len(cuts), largest / len(cuts))
        level = level * jnp.repeat(jnp.exp(steps), dims[dim] // blocks).reshape((-1,) + (1,) * (len(dims) - 1 - dim))
    return level


def normal_values(stream_key, extent, scale, bound, cuts=(), held_as=jnp.bfloat16):
    values = scale * jax.random.normal(stream_key, extent, jnp.float32)
    if cuts:
        values = values * block_scale(stream_key, extent, cuts, -0.22, 0.18)
    return jnp.clip(values, -bound, bound).astype(held_as)


def setup_inputs(seed: int = 0) -> dict:
    keys = jax.random.split(jax.random.key(seed), 8)
    return {
        "couplings": normal_values(keys[0], (BLOCKS, SLOTS, BAND, UNK, UNK), (4 * BAND * UNK) ** -0.5, 0.0625, ((0, 128),)),
        "history": normal_values(keys[1], (HIST, UNKNOWNS, EXC), 1.0, 6.0, ((1, 128),)),
        "diag_inverse": normal_values(keys[2], (BLOCKS, UNK, UNK), UNK ** -0.5, 0.25, ((0, 128),)),
        "incident": normal_values(keys[3], (STEPS, UNKNOWNS, EXC), 1.0, 6.0, ((1, 128),)),
        "targets": set_ends(jax.random.randint(keys[4], (BLOCKS, SLOTS), 0, 11), jax.random.fold_in(keys[4], 1), 0, 10).astype(jnp.int32),
        "delays": set_ends(jax.random.randint(keys[5], (BLOCKS, SLOTS), 1, HIST - BAND + 2), jax.random.fold_in(keys[5], 1), 1, (HIST - BAND + 2) - 1).astype(jnp.int32),
        "counts": draw_counts(jax.random.fold_in(keys[7], 71), 0),
    }


def code_offsets(target_code):
    if target_code < 5:
        return 0, target_code - 2
    if target_code < 8:
        return 1, target_code - 6
    return -1, target_code - 9


def reference(couplings, history, diag_inverse, incident, targets, delays, counts):
    recent = history
    outputs = []
    for moment in range(STEPS):
        def block_terms(block_id):
            matrices = couplings[block_id].astype(jnp.float32)
            block_rows = lax.dynamic_slice_in_dim(recent, block_id * UNK, UNK, 1)

            def take_band(lowest):
                return lax.dynamic_slice_in_dim(block_rows, (lowest - 1).astype(jnp.int32), BAND, 0)

            slices = jax.vmap(take_band)(delays[block_id]).astype(jnp.float32)
            product = jnp.einsum("cwij,cwjr->cir", matrices, slices, precision=lax.Precision.HIGHEST)
            live_slots = jnp.arange(SLOTS, dtype=jnp.int32) < counts[block_id]
            onehot = ((targets[block_id][None, :] == jnp.arange(11, dtype=jnp.int32)[:, None]) & live_slots[None, :]).astype(jnp.float32)
            return jnp.einsum("sc,cir->sir", onehot, product, precision=lax.Precision.HIGHEST)

        stencil = lax.map(block_terms, jnp.arange(BLOCKS, dtype=jnp.int32))
        stencil = stencil.reshape(N_GROUP, N_DEV, 11, UNK, EXC)
        padded = jnp.pad(stencil, ((1, 1), (2, 2), (0, 0), (0, 0), (0, 0)))
        field_sum = jnp.zeros((N_GROUP, N_DEV, UNK, EXC), jnp.float32)
        for target_code in range(11):
            grp_step, dev_step = code_offsets(target_code)
            field_sum = field_sum + padded[1 - grp_step:1 - grp_step + N_GROUP, 2 - dev_step:2 - dev_step + N_DEV, target_code]
        field_sum = field_sum.reshape(UNKNOWNS, EXC)
        right_side = (incident[moment].astype(jnp.float32) - field_sum).astype(jnp.bfloat16)
        blocks_rhs = right_side.reshape(BLOCKS, UNK, EXC).astype(jnp.float32)
        current = jnp.einsum("bij,bjr->bir", diag_inverse.astype(jnp.float32), blocks_rhs, precision=lax.Precision.HIGHEST)
        current = current.astype(jnp.bfloat16).reshape(UNKNOWNS, EXC)
        outputs.append(current)
        recent = jnp.concatenate([current[None], recent[:-1]], axis=0)
    return jnp.stack(outputs)
```

```python
import functools

import jax
import jax.numpy as jnp
from jax import lax
from jax.experimental import pallas as pl
from jax.experimental.pallas import tpu as pltpu
from jax.sharding import PartitionSpec as P

BAND = 4
STEPS = 2
LANES = 128
MESH = pl.DeviceIdType.MESH

FAR_R, FAR_L, UP, DOWN, SUM_R, SUM_L = 0, 1, 2, 5, 8, 9
KINDS = 10


def march_kernel(
    n_group,
    n_dev,
    targets,
    delays,
    counts,
    couplings,
    history,
    diag,
    incident,
    out,
    past,
    mats,
    solve,
    shine,
    product,
    terms,
    gated,
    far,
    near,
    cross,
    load_sem,
    mat_sem,
    send_sem,
    recv_sem,
):
    g = lax.axis_index("group")
    d = lax.axis_index("dev")
    slots = mats.shape[0]
    unk = mats.shape[2]
    halves = terms.shape[1]
    tile = min(unk, 128)
    has_up, has_down = g < n_group - 1, g > 0
    has_right, has_left = d < n_dev - 1, d > 0

    loads = [
        pltpu.make_async_copy(history.at[pl.ds(0, past.shape[0] - 1)], past.at[pl.ds(1, past.shape[0] - 1)], load_sem.at[0]),
        pltpu.make_async_copy(diag.at[0], solve, load_sem.at[1]),
        pltpu.make_async_copy(incident, shine, load_sem.at[2]),
    ]
    loads[0].start()

    def mat_load(c):
        return pltpu.make_async_copy(couplings.at[0, c], mats.at[c], mat_sem.at[c])

    @pl.loop(0, slots)
    def _(c):
        mat_load(c).start()

    loads[1].start()
    loads[2].start()

    barrier = pltpu.get_barrier_semaphore()
    partners = (
        (has_up, (g + 1, d)),
        (has_down, (g - 1, d)),
        (has_right, (g, d + 1)),
        (has_left, (g, d - 1)),
    )
    greeted = jnp.int32(0)
    for there, where in partners:

        @pl.when(there)
        def _():
            pl.semaphore_signal(barrier, inc=1, device_id=where, device_id_type=MESH)

        greeted = greeted + there.astype(jnp.int32)

    past[0] = jnp.zeros_like(past[0])
    gated[0] = jnp.zeros_like(gated[0])
    for side, absent in ((0, jnp.logical_not(has_down)), (1, jnp.logical_not(has_up))):

        @pl.when(absent)
        def _():
            for t in range(STEPS):
                for h in range(halves):
                    cross[t, h, side] = jnp.zeros_like(cross[t, h, side])

    for side, absent in ((0, jnp.logical_not(has_left)), (1, jnp.logical_not(has_right))):

        @pl.when(absent)
        def _():
            for t in range(STEPS):
                for h in range(halves):
                    far[t, h, side] = jnp.zeros_like(far[t, h, side])
                    near[t, h, side] = jnp.zeros_like(near[t, h, side])

    def remote(src, dst, t, h, kind, where):
        return pltpu.make_async_remote_copy(
            src_ref=src,
            dst_ref=dst,
            send_sem=send_sem.at[t, h, kind],
            recv_sem=recv_sem.at[t, h, kind],
            device_id=where,
            device_id_type=MESH,
        )

    def copies(t, h):
        st = terms.at[t, h]
        plan = {
            FAR_R: (remote(st.at[4], far.at[t, h, 0], t, h, FAR_R, (g, d + 1)), d < n_dev - 2, (d >= 1) & (d < n_dev - 1)),
            FAR_L: (remote(st.at[0], far.at[t, h, 1], t, h, FAR_L, (g, d - 1)), d >= 2, (d >= 1) & (d < n_dev - 1)),
            SUM_R: (remote(st.at[3], near.at[t, h, 0], t, h, SUM_R, (g, d + 1)), has_right, has_left),
            SUM_L: (remote(st.at[1], near.at[t, h, 1], t, h, SUM_L, (g, d - 1)), has_left, has_right),
        }
        for k in range(3):
            plan[UP + k] = (remote(st.at[5 + k], cross.at[t, h, 0, k], t, h, UP + k, (g + 1, d)), has_up, has_down)
            plan[DOWN + k] = (remote(st.at[8 + k], cross.at[t, h, 1, k], t, h, DOWN + k, (g - 1, d)), has_down, has_up)
        return plan

    plans = {(t, h): copies(t, h) for t in range(STEPS) for h in range(halves)}

    def send(t, h, kind):
        copy, sends, _ = plans[t, h][kind]

        @pl.when(sends)
        def _():
            copy.start()

    def arrive(t, h, kind):
        copy, _, hears = plans[t, h][kind]

        @pl.when(hears)
        def _():
            copy.wait_recv()

    live = [(jnp.int32(c) < counts[0]) for c in range(slots)]

    def weight(s, c):
        return jnp.where(live[c] & (targets[0, c] == s), 1.0, 0.0).astype(jnp.float32)

    def gather_terms(t, h, codes):
        weights = {s: [weight(s, c) for c in range(slots)] for s in codes}

        @pl.loop(0, unk // tile)
        def _(r):
            rows = pl.ds(pl.multiple_of(r * tile, tile), tile)
            parts = [product[c, h, rows, :] for c in range(slots)]
            for s in codes:
                total = parts[0] * weights[s][0]
                for c in range(1, slots):
                    total = total + parts[c] * weights[s][c]
                terms[t, h, s, rows, :] = total

    def launch(t, h):
        for codes, kinds in (
            ((4, 0), (FAR_R, FAR_L)),
            ((5, 7), (UP, UP + 2)),
            ((8, 10), (DOWN, DOWN + 2)),
            ((6, 9), (UP + 1, DOWN + 1)),
        ):
            gather_terms(t, h, codes)
            for kind in kinds:
                send(t, h, kind)
        gather_terms(t, h, (3, 1, 2))

    def products(shift):
        @pl.loop(0, slots)
        def _(c):
            if shift:
                mat_load(c).wait()
            first = jnp.maximum(delays[0, c], 1) - 1 + shift
            total = jnp.dot(mats[c, 0], past[first], preferred_element_type=jnp.float32)
            for w in range(1, BAND):
                total = total + jnp.dot(mats[c, w], past[first + w], preferred_element_type=jnp.float32)
            for h in range(halves):
                product[c, h] = total[:, h * LANES : (h + 1) * LANES]

    def pass_on(t, h):
        arrive(t, h, FAR_R)
        arrive(t, h, UP + 2)
        arrive(t, h, DOWN + 2)

        @pl.when(has_right)
        def _():
            terms[t, h, 3] = terms[t, h, 3] + cross[t, h, 0, 2] + cross[t, h, 1, 2] + far[t, h, 0]

        send(t, h, SUM_R)
        arrive(t, h, FAR_L)
        arrive(t, h, UP)
        arrive(t, h, DOWN)

        @pl.when(has_left)
        def _():
            terms[t, h, 1] = terms[t, h, 1] + cross[t, h, 0, 0] + cross[t, h, 1, 0] + far[t, h, 1]

        send(t, h, SUM_L)

    def finish(t, h):
        cols = pl.ds(h * LANES, LANES)
        for kind in (UP + 1, DOWN + 1, SUM_R, SUM_L):
            arrive(t, h, kind)
        field = terms[t, h, 2] + cross[t, h, 0, 1] + cross[t, h, 1, 1] + near[t, h, 0] + near[t, h, 1]
        right_side = (shine[t, :, cols].astype(jnp.float32) - field).astype(jnp.bfloat16)
        current = jnp.dot(solve[...], right_side, preferred_element_type=jnp.float32).astype(jnp.bfloat16)
        out[t, :, cols] = current
        if t == 0:
            gated[1] = current

            @pl.loop(0, slots)
            def _(c):
                fresh = jnp.where(delays[0, c] == 1, 1, 0)
                product[c, h] = product[c, h] + jnp.dot(mats[c, 0], gated[fresh], preferred_element_type=jnp.float32)

    loads[0].wait()
    pl.semaphore_wait(barrier, greeted)
    products(1)
    for h in range(halves):
        launch(0, h)
    products(0)
    for h in range(halves):
        pass_on(0, h)
    loads[1].wait()
    loads[2].wait()
    for h in range(halves):
        finish(0, h)
        launch(1, h)
    for h in range(halves):
        pass_on(1, h)
    for h in range(halves):
        finish(1, h)
    for plan in plans.values():
        for copy, sends, _ in plan.values():

            @pl.when(sends)
            def _():
                copy.wait_send()


def march(n_group, n_dev, couplings, history, diag_inverse, incident, targets, delays, counts):
    _, slots, band, unk, _ = couplings.shape
    hist, _, exc = history.shape
    halves = exc // LANES
    smem = pl.BlockSpec(memory_space=pltpu.SMEM)
    hbm = pl.BlockSpec(memory_space=pl.ANY)
    block = (unk, LANES)
    return pl.pallas_call(
        functools.partial(march_kernel, n_group, n_dev),
        out_shape=jax.ShapeDtypeStruct((STEPS, unk, exc), jnp.bfloat16),
        in_specs=[smem, smem, smem, hbm, hbm, hbm, hbm],
        out_specs=pl.BlockSpec(memory_space=pltpu.VMEM),
        scratch_shapes=[
            pltpu.VMEM((hist + 1, unk, exc), jnp.bfloat16),
            pltpu.VMEM((slots, band, unk, unk), jnp.bfloat16),
            pltpu.VMEM((unk, unk), jnp.bfloat16),
            pltpu.VMEM((STEPS, unk, exc), jnp.bfloat16),
            pltpu.VMEM((slots, halves) + block, jnp.float32),
            pltpu.VMEM((STEPS, halves, 11) + block, jnp.float32),
            pltpu.VMEM((2,) + block, jnp.bfloat16),
            pltpu.VMEM((STEPS, halves, 2) + block, jnp.float32),
            pltpu.VMEM((STEPS, halves, 2) + block, jnp.float32),
            pltpu.VMEM((STEPS, halves, 2, 3) + block, jnp.float32),
            pltpu.SemaphoreType.DMA((3,)),
            pltpu.SemaphoreType.DMA((slots,)),
            pltpu.SemaphoreType.DMA((STEPS, halves, KINDS)),
            pltpu.SemaphoreType.DMA((STEPS, halves, KINDS)),
        ],
        compiler_params=pltpu.CompilerParams(
            collective_id=0, has_side_effects=True, vmem_limit_bytes=62 * 2**20
        ),
        name="march",
    )(targets, delays, counts, couplings, history, diag_inverse, incident)


def solution(mesh):
    placed = (
        P(("group", "dev"), None, None, None, None),
        P(None, ("group", "dev"), None),
        P(("group", "dev"), None, None),
        P(None, ("group", "dev"), None),
        P(("group", "dev"), None),
        P(("group", "dev"), None),
        P(("group", "dev")),
    )
    return jax.shard_map(
        functools.partial(march, mesh.shape["group"], mesh.shape["dev"]),
        mesh=mesh,
        in_specs=placed,
        out_specs=P(None, ("group", "dev"), None),
        check_vma=False,
    )
```

```python
import functools

import jax
import jax.numpy as jnp
from jax import lax
from jax.experimental import pallas as pl
from jax.experimental.pallas import tpu as pltpu
from jax.sharding import PartitionSpec as P

BAND = 4
STEPS = 2
LANES = 128
RUN = 4
MESH = pl.DeviceIdType.MESH

FAR_R, FAR_L, SUM_R, SUM_L, CHIP, JOIN, SKIP, MIDDLE = range(8)
KINDS = 8


def march_kernel(
    n_dev,
    run,
    targets,
    delays,
    counts,
    couplings,
    history,
    diag,
    incident,
    out,
    past,
    mats,
    solve,
    shine,
    product,
    terms,
    gated,
    box,
    chip_box,
    load_sem,
    mat_sem,
    send_sem,
    recv_sem,
):
    g = lax.axis_index("group")
    d = lax.axis_index("dev")
    slots = mats.shape[0]
    unk = mats.shape[2]
    halves = terms.shape[1]
    tile = min(unk, 128)
    has_right, has_left = d < n_dev - 1, d > 0
    mate = g + 1 - 2 * (g % 2)
    crosses = (g == 1) | (g == 2)
    over = 3 - g
    x = d % run
    chip_code = 5 + 3 * (g % 2)
    over_code = 5 + 3 * (g // 2)
    even = x % 2 == 0
    join_code = over_code + jnp.where(even, 2, 0)
    skip_code = over_code + jnp.where(even, 0, 2)
    join_dev = d + jnp.where(even, 1, -1)
    at_start, at_end = x == 0, x == run - 1
    skip_dev = d + jnp.where(at_start, -1, 0) + jnp.where(at_end, 1, 0)
    skips = crosses & (skip_dev >= 0) & (skip_dev < n_dev)
    at_rim = at_start | at_end
    skip_into = jnp.where(at_rim, 2, jnp.where(even, 1, 3))

    depth = past.shape[0] - 1
    loads = [
        pltpu.make_async_copy(history, past.at[pl.ds(1, depth)], load_sem.at[0]),
        pltpu.make_async_copy(diag.at[0], solve, load_sem.at[1]),
        pltpu.make_async_copy(incident, shine, load_sem.at[2]),
    ]
    loads[0].start()

    def mat_load(c):
        return pltpu.make_async_copy(couplings.at[0, c], mats.at[c], mat_sem.at[c])

    @pl.loop(0, slots)
    def _(c):
        mat_load(c).start()

    loads[1].start()
    loads[2].start()

    barrier = pltpu.get_barrier_semaphore()
    greeted = jnp.int32(1)
    pl.semaphore_signal(barrier, inc=1, device_id=(mate, d), device_id_type=MESH)
    for there, where in (
        (has_right, (g, d + 1)),
        (has_left, (g, d - 1)),
        (crosses, (over, d)),
        (skips & at_rim, (over, skip_dev)),
    ):

        @pl.when(there)
        def _():
            pl.semaphore_signal(barrier, inc=1, device_id=where, device_id_type=MESH)

        greeted = greeted + there.astype(jnp.int32)

    past[0] = jnp.zeros_like(past[0])
    gated[0] = jnp.zeros_like(gated[0])

    def remote(src, dst, t, h, kind, where):
        return pltpu.make_async_remote_copy(
            src_ref=src,
            dst_ref=dst,
            send_sem=send_sem.at[t, h, kind],
            recv_sem=recv_sem.at[t, h, kind],
            device_id=where,
            device_id_type=MESH,
        )

    def copies(t, h):
        def one(code, kind, where, sends, hears):
            return remote(terms.at[t, h, code], box.at[t, h, kind], t, h, kind, where), sends, hears

        inner = has_right & has_left
        chip = remote(terms.at[t, h, pl.ds(chip_code, 3)], chip_box.at[t, h], t, h, CHIP, (mate, d))
        return {
            FAR_R: one(4, FAR_R, (g, d + 1), d < n_dev - 2, inner),
            FAR_L: one(0, FAR_L, (g, d - 1), d >= 2, inner),
            SUM_R: one(3, SUM_R, (g, d + 1), has_right, has_left),
            SUM_L: one(1, SUM_L, (g, d - 1), has_left, has_right),
            CHIP: (chip, None, None),
            JOIN: one(join_code, JOIN, (g, join_dev), crosses, crosses),
            SKIP: one(skip_code, SKIP, (over, skip_dev), skips, skips),
            MIDDLE: one(over_code + 1, MIDDLE, (over, d), crosses, crosses),
        }

    plans = {(t, h): copies(t, h) for t in range(STEPS) for h in range(halves)}

    def when(there, do):
        if there is None:
            do()
        else:
            pl.when(there)(do)

    def send(t, h, kind):
        copy, sends, _ = plans[t, h][kind]
        when(sends, copy.start)

    def arrive(t, h, kind):
        copy, _, hears = plans[t, h][kind]
        when(hears, copy.wait_recv)

    live = [(jnp.int32(c) < counts[0]) for c in range(slots)]

    def weight(s, c):
        return jnp.where(live[c] & (targets[0, c] == s), 1.0, 0.0).astype(jnp.float32)

    def gather_terms(t, h, codes):
        weights = {s: [weight(s, c) for c in range(slots)] for s in codes}

        @pl.loop(0, unk // tile)
        def _(r):
            rows = pl.ds(pl.multiple_of(r * tile, tile), tile)
            parts = [product[c, h, rows, :] for c in range(slots)]
            for s in codes:
                total = parts[0] * weights[s][0]
                for c in range(1, slots):
                    total = total + parts[c] * weights[s][c]
                terms[t, h, s, rows, :] = total

    def launch(t, h):
        gather_terms(t, h, (4, 0))
        send(t, h, FAR_R)
        send(t, h, FAR_L)
        gather_terms(t, h, (5, 6, 7))
        gather_terms(t, h, (8, 9, 10))
        for kind in (JOIN, SKIP, CHIP):
            send(t, h, kind)
        gather_terms(t, h, (3, 1, 2))

    def products(shift):
        @pl.loop(0, slots)
        def _(c):
            if shift:
                mat_load(c).wait()
            first = jnp.maximum(delays[0, c], 1) - 1 + shift
            total = jnp.dot(mats[c, 0], past[first], preferred_element_type=jnp.float32)
            for w in range(1, BAND):
                total = total + jnp.dot(mats[c, w], past[first + w], preferred_element_type=jnp.float32)
            for h in range(halves):
                product[c, h] = total[:, h * LANES : (h + 1) * LANES]

    def add(t, h, code, kind, there):
        def do():
            terms[t, h, code] = terms[t, h, code] + box[t, h, kind]

        when(there, do)

    def pass_on(t, h):
        arrive(t, h, JOIN)
        add(t, h, over_code + 1, JOIN, crosses)
        send(t, h, MIDDLE)
        arrive(t, h, CHIP)
        arrive(t, h, SKIP)
        add(t, h, skip_into, SKIP, skips)
        for code, far_kind, sum_kind, sends in ((3, FAR_R, SUM_R, has_right), (1, FAR_L, SUM_L, has_left)):
            arrive(t, h, far_kind)
            terms[t, h, code] = terms[t, h, code] + chip_box[t, h, code - 1]
            add(t, h, code, far_kind, has_right & has_left)
            send(t, h, sum_kind)

    def finish(t, h):
        cols = pl.ds(h * LANES, LANES)
        terms[t, h, 2] = terms[t, h, 2] + chip_box[t, h, 1]
        for kind, there in ((MIDDLE, crosses), (SUM_R, has_left), (SUM_L, has_right)):
            arrive(t, h, kind)
            add(t, h, 2, kind, there)
        right_side = (shine[t, :, cols].astype(jnp.float32) - terms[t, h, 2]).astype(jnp.bfloat16)
        current = jnp.dot(solve[...], right_side, preferred_element_type=jnp.float32).astype(jnp.bfloat16)
        out[t, :, cols] = current
        if t == 0:
            gated[1] = current

            @pl.loop(0, slots)
            def _(c):
                fresh = jnp.where(delays[0, c] == 1, 1, 0)
                product[c, h] = product[c, h] + jnp.dot(mats[c, 0], gated[fresh], preferred_element_type=jnp.float32)

    loads[0].wait()
    pl.semaphore_wait(barrier, greeted)
    products(1)
    for h in range(halves):
        launch(0, h)
    products(0)
    for h in range(halves):
        pass_on(0, h)
    loads[1].wait()
    loads[2].wait()
    for h in range(halves):
        finish(0, h)
        launch(1, h)
    for h in range(halves):
        pass_on(1, h)
    for h in range(halves):
        finish(1, h)
    for plan in plans.values():
        for copy, sends, _ in plan.values():
            when(sends, copy.wait_send)


def march(n_dev, couplings, history, diag_inverse, incident, targets, delays, counts):
    _, slots, band, unk, _ = couplings.shape
    hist, _, exc = history.shape
    halves = exc // LANES
    smem = pl.BlockSpec(memory_space=pltpu.SMEM)
    hbm = pl.BlockSpec(memory_space=pl.ANY)
    block = (unk, LANES)
    return pl.pallas_call(
        functools.partial(march_kernel, n_dev, RUN),
        out_shape=jax.ShapeDtypeStruct((STEPS, unk, exc), jnp.bfloat16),
        in_specs=[smem, smem, smem, hbm, hbm, hbm, hbm],
        out_specs=pl.BlockSpec(memory_space=pltpu.VMEM),
        scratch_shapes=[
            pltpu.VMEM((hist + 1, unk, exc), jnp.bfloat16),
            pltpu.VMEM((slots, band, unk, unk), jnp.bfloat16),
            pltpu.VMEM((unk, unk), jnp.bfloat16),
            pltpu.VMEM((STEPS, unk, exc), jnp.bfloat16),
            pltpu.VMEM((slots, halves) + block, jnp.float32),
            pltpu.VMEM((STEPS, halves, 11) + block, jnp.float32),
            pltpu.VMEM((2,) + block, jnp.bfloat16),
            pltpu.VMEM((STEPS, halves, KINDS) + block, jnp.float32),
            pltpu.VMEM((STEPS, halves, 3) + block, jnp.float32),
            pltpu.SemaphoreType.DMA((3,)),
            pltpu.SemaphoreType.DMA((slots,)),
            pltpu.SemaphoreType.DMA((STEPS, halves, KINDS)),
            pltpu.SemaphoreType.DMA((STEPS, halves, KINDS)),
        ],
        compiler_params=pltpu.CompilerParams(
            collective_id=0, has_side_effects=True, vmem_limit_bytes=62 * 2**20
        ),
        name="march",
    )(targets, delays, counts, couplings, history, diag_inverse, incident)


def solution(mesh):
    placed = (
        P(("group", "dev"), None, None, None, None),
        P(None, ("group", "dev"), None),
        P(("group", "dev"), None, None),
        P(None, ("group", "dev"), None),
        P(("group", "dev"), None),
        P(("group", "dev"), None),
        P(("group", "dev")),
    )
    return jax.shard_map(
        functools.partial(march, mesh.shape["dev"]),
        mesh=mesh,
        in_specs=placed,
        out_specs=P(None, ("group", "dev"), None),
        check_vma=False,
    )
```

```python
import functools

import jax
import jax.numpy as jnp
from jax import lax
from jax.experimental import pallas as pl
from jax.experimental.pallas import tpu as pltpu
from jax.sharding import PartitionSpec as P

BAND = 4
STEPS = 2
LANES = 128
TILE = 128
RUN = 4
MESH = pl.DeviceIdType.MESH

FAR, SUM, CHIP, JOIN, SKIP, MIDDLE = 0, 2, 4, 5, 6, 7
KINDS = 8


def march_kernel(
    n_dev,
    run,
    targets,
    delays,
    counts,
    couplings,
    history,
    diag,
    incident,
    out,
    past_0,
    past_1,
    mats,
    solve,
    shine,
    product,
    terms,
    gated,
    box,
    chip_box,
    load_sem,
    mat_sem,
    send_sem,
    recv_sem,
):
    g = lax.axis_index("group")
    d = lax.axis_index("dev")
    slots = mats.shape[0]
    unk = mats.shape[2]
    halves = terms.shape[1]
    tiles = unk // TILE
    has_right, has_left = d < n_dev - 1, d > 0
    mate = g + 1 - 2 * (g % 2)
    crosses = (g == 1) | (g == 2)
    over = 3 - g
    x = d % run
    chip_code = 5 + 3 * (g % 2)
    over_code = 5 + 3 * (g // 2)
    even = x % 2 == 0
    join_code = over_code + jnp.where(even, 2, 0)
    skip_code = over_code + jnp.where(even, 0, 2)
    join_dev = d + jnp.where(even, 1, -1)
    at_start, at_end = x == 0, x == run - 1
    skip_dev = d + jnp.where(at_start, -1, 0) + jnp.where(at_end, 1, 0)
    skips = crosses & (skip_dev >= 0) & (skip_dev < n_dev)
    at_rim = at_start | at_end
    near_side = jnp.where(at_start, 1, 0)
    skip_into = jnp.where(at_rim, 2, jnp.where(even, 1, 3))

    def tile_rows(r):
        return pl.ds(pl.multiple_of(r * TILE, TILE), TILE)

    past = (past_0, past_1)
    depth = past_0.shape[0] - 1

    def history_load(h):
        cols = pl.ds(h * LANES, LANES)
        return pltpu.make_async_copy(history.at[:, :, cols], past[h].at[pl.ds(1, depth)], load_sem.at[h])

    solve_load = pltpu.make_async_copy(diag.at[0], solve, load_sem.at[halves])
    shine_load = pltpu.make_async_copy(incident, shine, load_sem.at[halves + 1])

    def mat_load(r):
        rows = tile_rows(r)
        return pltpu.make_async_copy(couplings.at[0, :, :, rows, :], mats.at[:, :, rows, :], mat_sem.at[r])

    history_load(0).start()
    mat_load(0).start()
    for h in range(1, halves):
        history_load(h).start()

    @pl.loop(1, tiles)
    def _(r):
        mat_load(r).start()

    solve_load.start()
    shine_load.start()

    barrier = pltpu.get_barrier_semaphore()
    greeted = jnp.int32(1)
    pl.semaphore_signal(barrier, inc=1, device_id=(mate, d), device_id_type=MESH)
    for there, where in (
        (has_right, (g, d + 1)),
        (has_left, (g, d - 1)),
        (crosses, (over, d)),
        (skips & at_rim, (over, skip_dev)),
    ):

        @pl.when(there)
        def _():
            pl.semaphore_signal(barrier, inc=1, device_id=where, device_id_type=MESH)

        greeted = greeted + there.astype(jnp.int32)

    for held in past:
        held[0] = jnp.zeros_like(held[0])
    gated[0] = jnp.zeros_like(gated[0])

    def copy_of(t, h, r, kind, side=0):
        code_is_chip = kind == CHIP
        inner = has_right & has_left
        aside = d + 1 - 2 * side
        beyond = aside + 1 - 2 * side
        inside = (aside >= 0) & (aside < n_dev)
        behind = d - 1 + 2 * side
        code, where, sends, hears = {
            FAR: (4 - 4 * side, (g, aside), (beyond >= 0) & (beyond < n_dev), inner),
            SUM: (3 - 2 * side, (g, aside), inside, (behind >= 0) & (behind < n_dev)),
            CHIP: (pl.ds(chip_code, 3), (mate, d), None, None),
            JOIN: (join_code, (g, join_dev), crosses, crosses),
            SKIP: (skip_code, (over, skip_dev), skips, skips),
            MIDDLE: (over_code + 1, (over, d), crosses, crosses),
        }[kind]
        rows = tile_rows(r)
        kind = kind + side
        target = chip_box.at[t, h, :, rows] if code_is_chip else box.at[t, h, kind, rows]
        copy = pltpu.make_async_remote_copy(
            src_ref=terms.at[t, h, code, rows],
            dst_ref=target,
            send_sem=send_sem.at[t, h, kind, r],
            recv_sem=recv_sem.at[t, h, kind, r],
            device_id=where,
            device_id_type=MESH,
        )
        return copy, sends, hears

    def when(there, do):
        if there is None:
            do()
        else:
            pl.when(there)(do)

    def send(t, h, r, kind, side=0):
        copy, sends, _ = copy_of(t, h, r, kind, side)
        when(sends, copy.start)

    def arrive(t, h, r, kind, side=0):
        copy, _, hears = copy_of(t, h, r, kind, side)
        when(hears, copy.wait_recv)

    live = [(jnp.int32(c) < counts[0]) for c in range(slots)]

    def weight(s, c):
        return jnp.where(live[c] & (targets[0, c] == s), 1.0, 0.0).astype(jnp.float32)

    weights = [[weight(s, c) for c in range(slots)] for s in range(11)]

    def gather_terms(t, h, r, codes):
        rows = tile_rows(r)
        parts = [product[c, h, rows, :] for c in range(slots)]
        for s in codes:
            total = parts[0] * weights[s][0]
            for c in range(1, slots):
                total = total + parts[c] * weights[s][c]
            terms[t, h, s, rows, :] = total

    def launch(t, h, r):
        gather_terms(t, h, r, (5, 6, 7))
        gather_terms(t, h, r, (8, 9, 10))
        for kind in (JOIN, SKIP, CHIP):
            send(t, h, r, kind)
        gather_terms(t, h, r, (4, 0))
        for side in (0, 1):
            send(t, h, r, FAR, side)
        gather_terms(t, h, r, (3, 1, 2))

    def first_of(c):
        return jnp.maximum(delays[0, c], 1) - 1

    def products(shift, rows, over_halves):
        def taken(at):
            return jnp.concatenate([past[h][at] for h in over_halves], axis=1)

        @pl.loop(0, slots)
        def _(c):
            first = first_of(c) + shift
            total = jnp.dot(mats[c, 0, rows], taken(first), preferred_element_type=jnp.float32)
            for w in range(1, BAND):
                total = total + jnp.dot(mats[c, w, rows], taken(first + w), preferred_element_type=jnp.float32)
            for i, h in enumerate(over_halves):
                product[c, h, rows, :] = total[:, i * LANES : (i + 1) * LANES]

    def add(t, h, r, code, kind, there):
        rows = tile_rows(r)

        def do():
            terms[t, h, code, rows] = terms[t, h, code, rows] + box[t, h, kind, rows]

        when(there, do)

    def join(t, h, r):
        arrive(t, h, r, JOIN)
        add(t, h, r, over_code + 1, JOIN, crosses)
        send(t, h, r, MIDDLE)

    def pass_on(t, h, r):
        rows = tile_rows(r)
        arrive(t, h, r, CHIP)
        arrive(t, h, r, SKIP)
        add(t, h, r, skip_into, SKIP, skips)
        for side in (near_side, 1 - near_side):
            code = 3 - 2 * side
            arrive(t, h, r, FAR, side)
            terms[t, h, code, rows] = terms[t, h, code, rows] + chip_box[t, h, code - 1, rows]
            add(t, h, r, code, FAR + side, has_right & has_left)
            send(t, h, r, SUM, side)

    def solve_step(t, h):
        cols = pl.ds(h * LANES, LANES)

        @pl.loop(0, tiles)
        def _(r):
            rows = tile_rows(r)
            terms[t, h, 2, rows] = terms[t, h, 2, rows] + chip_box[t, h, 1, rows]
            for kind, side, there in ((MIDDLE, 0, crosses), (SUM, 0, has_left), (SUM, 1, has_right)):
                arrive(t, h, r, kind, side)
                add(t, h, r, 2, kind + side, there)

        right_side = (shine[t, :, cols].astype(jnp.float32) - terms[t, h, 2]).astype(jnp.bfloat16)
        current = jnp.dot(solve[...], right_side, preferred_element_type=jnp.float32).astype(jnp.bfloat16)
        out[t, :, cols] = current
        if t == 0:
            gated[1] = current

    def refresh(h, rows):
        @pl.loop(0, slots)
        def _(c):
            fresh = jnp.where(delays[0, c] == 1, 1, 0)
            product[c, h, rows] = product[c, h, rows] + jnp.dot(mats[c, 0, rows], gated[fresh], preferred_element_type=jnp.float32)

    every = list(range(halves))
    history_load(0).wait()
    mat_load(0).wait()
    products(1, tile_rows(0), every[:1])
    pl.semaphore_wait(barrier, greeted)
    launch(0, 0, 0)
    for h in every[1:]:
        history_load(h).wait()
        products(1, tile_rows(0), [h])
        launch(0, h, 0)

    @pl.loop(1, tiles)
    def _(r):
        mat_load(r).wait()
        products(1, tile_rows(r), every)
        for h in every:
            launch(0, h, r)
            join(0, h, r - 1)

    for h in every:
        join(0, h, tiles - 1)

    @pl.loop(0, tiles)
    def _(r):
        pass_on(0, 0, r)
        products(0, tile_rows(r), every)

    for h in every[1:]:

        @pl.loop(0, tiles)
        def _(r):
            pass_on(0, h, r)

    solve_load.wait()
    shine_load.wait()
    for h in every:
        solve_step(0, h)

        @pl.loop(0, tiles)
        def _(r):
            refresh(h, tile_rows(r))
            launch(1, h, r)

            @pl.when(r > 0)
            def _():
                join(1, h, r - 1)

            if h:
                pass_on(1, h - 1, r)

        join(1, h, tiles - 1)

    @pl.loop(0, tiles)
    def _(r):
        pass_on(1, halves - 1, r)

    for h in every:
        solve_step(1, h)
    for t in range(STEPS):
        for h in range(halves):

            @pl.loop(0, tiles)
            def _(r):
                for kind, side in ((FAR, 0), (FAR, 1), (SUM, 0), (SUM, 1), (CHIP, 0), (JOIN, 0), (SKIP, 0), (MIDDLE, 0)):
                    copy, sends, _ = copy_of(t, h, r, kind, side)
                    when(sends, copy.wait_send)


def march(n_dev, couplings, history, diag_inverse, incident, targets, delays, counts):
    _, slots, band, unk, _ = couplings.shape
    hist, _, exc = history.shape
    halves = exc // LANES
    smem = pl.BlockSpec(memory_space=pltpu.SMEM)
    hbm = pl.BlockSpec(memory_space=pl.ANY)
    block = (unk, LANES)
    return pl.pallas_call(
        functools.partial(march_kernel, n_dev, RUN),
        out_shape=jax.ShapeDtypeStruct((STEPS, unk, exc), jnp.bfloat16),
        in_specs=[smem, smem, smem, hbm, hbm, hbm, hbm],
        out_specs=pl.BlockSpec(memory_space=pltpu.VMEM),
        scratch_shapes=[
            pltpu.VMEM((hist + 1,) + block, jnp.bfloat16),
            pltpu.VMEM((hist + 1,) + block, jnp.bfloat16),
            pltpu.VMEM((slots, band, unk, unk), jnp.bfloat16),
            pltpu.VMEM((unk, unk), jnp.bfloat16),
            pltpu.VMEM((STEPS, unk, exc), jnp.bfloat16),
            pltpu.VMEM((slots, halves) + block, jnp.float32),
            pltpu.VMEM((STEPS, halves, 11) + block, jnp.float32),
            pltpu.VMEM((2,) + block, jnp.bfloat16),
            pltpu.VMEM((STEPS, halves, KINDS) + block, jnp.float32),
            pltpu.VMEM((STEPS, halves, 3) + block, jnp.float32),
            pltpu.SemaphoreType.DMA((halves + 2,)),
            pltpu.SemaphoreType.DMA((unk // TILE,)),
            pltpu.SemaphoreType.DMA((STEPS, halves, KINDS, unk // TILE)),
            pltpu.SemaphoreType.DMA((STEPS, halves, KINDS, unk // TILE)),
        ],
        compiler_params=pltpu.CompilerParams(
            collective_id=0, has_side_effects=True, vmem_limit_bytes=62 * 2**20
        ),
        name="march",
    )(targets, delays, counts, couplings, history, diag_inverse, incident)


def solution(mesh):
    placed = (
        P(("group", "dev"), None, None, None, None),
        P(None, ("group", "dev"), None),
        P(("group", "dev"), None, None),
        P(None, ("group", "dev"), None),
        P(("group", "dev"), None),
        P(("group", "dev"), None),
        P(("group", "dev")),
    )
    return jax.shard_map(
        functools.partial(march, mesh.shape["dev"]),
        mesh=mesh,
        in_specs=placed,
        out_specs=P(None, ("group", "dev"), None),
        check_vma=False,
    )
```

```python
import functools

import jax
import jax.numpy as jnp
from jax import lax
from jax.experimental import pallas as pl
from jax.experimental.pallas import tpu as pltpu
from jax.sharding import PartitionSpec as P

BAND = 4
STEPS = 2
LANES = 128
TILE = 128
RUN = 4
MESH = pl.DeviceIdType.MESH

FAR, SUM, CHIP, JOIN, SKIP, MIDDLE, SIDE = 0, 2, 4, 5, 6, 7, 8
KINDS = 9


def march_kernel(
    n_dev,
    run,
    targets,
    delays,
    counts,
    couplings,
    history,
    diag,
    incident,
    out,
    past_0,
    past_1,
    mats,
    solve,
    shine,
    product,
    terms,
    gated,
    box,
    chip_box,
    load_sem,
    mat_sem,
    send_sem,
    recv_sem,
):
    g = lax.axis_index("group")
    d = lax.axis_index("dev")
    slots = mats.shape[0]
    unk = mats.shape[2]
    halves = terms.shape[1]
    tiles = unk // TILE
    has_right, has_left = d < n_dev - 1, d > 0
    mate = g + 1 - 2 * (g % 2)
    crosses = (g == 1) | (g == 2)
    over = 3 - g
    x = d % run
    chip_code = 5 + 3 * (g % 2)
    over_code = 5 + 3 * (g // 2)
    even = x % 2 == 0
    at_start, at_end = x == 0, x == run - 1
    at_rim = at_start | at_end
    join_code = over_code + jnp.where(even, 2, 0)
    skip_code = over_code + jnp.where(even, 0, 2)
    join_group = jnp.where(at_rim, g, over)
    join_dev = d + jnp.where(at_start, 1, 0) - jnp.where(at_end, 1, 0)
    skip_dev = d - jnp.where(at_start, 1, 0) + jnp.where(at_end, 1, 0)
    skips = crosses & (skip_dev >= 0) & (skip_dev < n_dev)
    gathers = crosses & jnp.logical_not(at_rim)
    skip_into = jnp.where(at_rim, 2, jnp.where(even, 1, 3))
    side_into = jnp.where(even, 3, 1)
    near_side = jnp.where(at_start, 1, 0)
    skip_into = jnp.where(at_rim, 2, jnp.where(even, 1, 3))

    def tile_rows(r):
        return pl.ds(pl.multiple_of(r * TILE, TILE), TILE)

    past = (past_0, past_1)
    depth = past_0.shape[0] - 1

    def history_load(h):
        cols = pl.ds(h * LANES, LANES)
        return pltpu.make_async_copy(history.at[:, :, cols], past[h].at[pl.ds(1, depth)], load_sem.at[h])

    solve_load = pltpu.make_async_copy(diag.at[0], solve, load_sem.at[halves])
    shine_load = pltpu.make_async_copy(incident, shine, load_sem.at[halves + 1])

    def mat_load(r):
        rows = tile_rows(r)
        return pltpu.make_async_copy(couplings.at[0, :, :, rows, :], mats.at[:, :, rows, :], mat_sem.at[r])

    history_load(0).start()
    mat_load(0).start()
    for h in range(1, halves):
        history_load(h).start()

    @pl.loop(1, tiles)
    def _(r):
        mat_load(r).start()

    solve_load.start()
    shine_load.start()

    barrier = pltpu.get_barrier_semaphore()
    greeted = jnp.int32(1)
    pl.semaphore_signal(barrier, inc=1, device_id=(mate, d), device_id_type=MESH)
    for there, where in (
        (has_right, (g, d + 1)),
        (has_left, (g, d - 1)),
        (crosses, (over, d)),
        (skips & at_rim, (over, skip_dev)),
    ):

        @pl.when(there)
        def _():
            pl.semaphore_signal(barrier, inc=1, device_id=where, device_id_type=MESH)

        greeted = greeted + there.astype(jnp.int32)

    for held in past:
        held[0] = jnp.zeros_like(held[0])
    gated[0] = jnp.zeros_like(gated[0])

    def copy_of(t, h, r, kind, side=0, leaving=False):
        code_is_chip = kind == CHIP
        inner = has_right & has_left
        aside = d + 1 - 2 * side
        beyond = aside + 1 - 2 * side
        inside = (aside >= 0) & (aside < n_dev)
        behind = d - 1 + 2 * side
        code, where, sends, hears = {
            FAR: (4 - 4 * side, (g, aside), (beyond >= 0) & (beyond < n_dev), inner),
            SUM: (3 - 2 * side, (g, aside), inside, (behind >= 0) & (behind < n_dev)),
            CHIP: (pl.ds(chip_code, 3), (mate, d), None, None),
            JOIN: (join_code, (join_group, join_dev), crosses, gathers),
            SIDE: (join_code, (join_group, join_dev), crosses, gathers),
            SKIP: (skip_code, (over, skip_dev), skips, skips),
            MIDDLE: (over_code + 1, (over, d), crosses, crosses),
        }[kind]
        rows = tile_rows(r)
        kind = jnp.where(at_rim, JOIN, SIDE) if leaving and kind == JOIN else kind + side
        target = chip_box.at[t, h, :, rows] if code_is_chip else box.at[t, h, kind, rows]
        copy = pltpu.make_async_remote_copy(
            src_ref=terms.at[t, h, code, rows],
            dst_ref=target,
            send_sem=send_sem.at[t, h, kind, r],
            recv_sem=recv_sem.at[t, h, kind, r],
            device_id=where,
            device_id_type=MESH,
        )
        return copy, sends, hears

    def when(there, do):
        if there is None:
            do()
        else:
            pl.when(there)(do)

    def send(t, h, r, kind, side=0):
        copy, sends, _ = copy_of(t, h, r, kind, side, True)
        when(sends, copy.start)

    def arrive(t, h, r, kind, side=0):
        copy, _, hears = copy_of(t, h, r, kind, side)
        when(hears, copy.wait_recv)

    live = [(jnp.int32(c) < counts[0]) for c in range(slots)]

    def weight(s, c):
        return jnp.where(live[c] & (targets[0, c] == s), 1.0, 0.0).astype(jnp.float32)

    weights = [[weight(s, c) for c in range(slots)] for s in range(11)]

    def gather_terms(t, h, r, codes):
        rows = tile_rows(r)
        parts = [product[c, h, rows, :] for c in range(slots)]
        for s in codes:
            total = parts[0] * weights[s][0]
            for c in range(1, slots):
                total = total + parts[c] * weights[s][c]
            terms[t, h, s, rows, :] = total

    def launch(t, h, r):
        gather_terms(t, h, r, (5, 6, 7))
        gather_terms(t, h, r, (8, 9, 10))
        for kind in (JOIN, SKIP, CHIP):
            send(t, h, r, kind)

        @pl.when(at_rim)
        def _():
            send(t, h, r, MIDDLE)

        gather_terms(t, h, r, (4, 0))
        for side in (0, 1):
            send(t, h, r, FAR, side)
        gather_terms(t, h, r, (3, 1, 2))

    def first_of(c):
        return jnp.maximum(delays[0, c], 1) - 1

    def products(shift, rows, over_halves):
        def taken(at):
            return jnp.concatenate([past[h][at] for h in over_halves], axis=1)

        @pl.loop(0, slots)
        def _(c):
            first = first_of(c) + shift
            total = jnp.dot(mats[c, 0, rows], taken(first), preferred_element_type=jnp.float32)
            for w in range(1, BAND):
                total = total + jnp.dot(mats[c, w, rows], taken(first + w), preferred_element_type=jnp.float32)
            for i, h in enumerate(over_halves):
                product[c, h, rows, :] = total[:, i * LANES : (i + 1) * LANES]

    def add(t, h, r, code, kind, there):
        rows = tile_rows(r)

        def do():
            terms[t, h, code, rows] = terms[t, h, code, rows] + box[t, h, kind, rows]

        when(there, do)

    def join(t, h, r):
        @pl.when(gathers)
        def _():
            arrive(t, h, r, JOIN)
            add(t, h, r, over_code + 1, JOIN, None)
            send(t, h, r, MIDDLE)

    def pass_on(t, h, r):
        rows = tile_rows(r)
        arrive(t, h, r, CHIP)
        arrive(t, h, r, SKIP)
        add(t, h, r, skip_into, SKIP, skips)
        arrive(t, h, r, SIDE)
        add(t, h, r, side_into, SIDE, gathers)
        for side in (near_side, 1 - near_side):
            code = 3 - 2 * side
            arrive(t, h, r, FAR, side)
            terms[t, h, code, rows] = terms[t, h, code, rows] + chip_box[t, h, code - 1, rows]
            add(t, h, r, code, FAR + side, has_right & has_left)
            send(t, h, r, SUM, side)

    def solve_step(t, h):
        cols = pl.ds(h * LANES, LANES)

        @pl.loop(0, tiles)
        def _(r):
            rows = tile_rows(r)
            terms[t, h, 2, rows] = terms[t, h, 2, rows] + chip_box[t, h, 1, rows]
            for kind, side, there in ((MIDDLE, 0, crosses), (SUM, 0, has_left), (SUM, 1, has_right)):
                arrive(t, h, r, kind, side)
                add(t, h, r, 2, kind + side, there)

        right_side = (shine[t, :, cols].astype(jnp.float32) - terms[t, h, 2]).astype(jnp.bfloat16)
        current = jnp.dot(solve[...], right_side, preferred_element_type=jnp.float32).astype(jnp.bfloat16)
        out[t, :, cols] = current
        if t == 0:
            gated[1] = current

    def refresh(h, rows):
        @pl.loop(0, slots)
        def _(c):
            fresh = jnp.where(delays[0, c] == 1, 1, 0)
            product[c, h, rows] = product[c, h, rows] + jnp.dot(mats[c, 0, rows], gated[fresh], preferred_element_type=jnp.float32)

    every = list(range(halves))
    history_load(0).wait()
    mat_load(0).wait()
    products(1, tile_rows(0), every[:1])
    pl.semaphore_wait(barrier, greeted)
    launch(0, 0, 0)
    for h in every[1:]:
        history_load(h).wait()
        products(1, tile_rows(0), [h])
        launch(0, h, 0)

    @pl.loop(1, tiles)
    def _(r):
        mat_load(r).wait()
        products(1, tile_rows(r), every)
        for h in every:
            launch(0, h, r)
            join(0, h, r - 1)

    for h in every:
        join(0, h, tiles - 1)

    @pl.loop(0, tiles)
    def _(r):
        pass_on(0, 0, r)
        products(0, tile_rows(r), every)

    for h in every[1:]:

        @pl.loop(0, tiles)
        def _(r):
            pass_on(0, h, r)

    solve_load.wait()
    shine_load.wait()
    for h in every:
        solve_step(0, h)

        @pl.loop(0, tiles)
        def _(r):
            refresh(h, tile_rows(r))
            launch(1, h, r)

            @pl.when(r > 0)
            def _():
                join(1, h, r - 1)

            if h:
                pass_on(1, h - 1, r)

        join(1, h, tiles - 1)

    @pl.loop(0, tiles)
    def _(r):
        pass_on(1, halves - 1, r)

    for h in every:
        solve_step(1, h)
    for t in range(STEPS):
        for h in range(halves):

            @pl.loop(0, tiles)
            def _(r):
                for kind, side in ((FAR, 0), (FAR, 1), (SUM, 0), (SUM, 1), (CHIP, 0), (JOIN, 0), (SKIP, 0), (MIDDLE, 0)):
                    copy, sends, _ = copy_of(t, h, r, kind, side, True)
                    when(sends, copy.wait_send)


def march(n_dev, couplings, history, diag_inverse, incident, targets, delays, counts):
    _, slots, band, unk, _ = couplings.shape
    hist, _, exc = history.shape
    halves = exc // LANES
    smem = pl.BlockSpec(memory_space=pltpu.SMEM)
    hbm = pl.BlockSpec(memory_space=pl.ANY)
    block = (unk, LANES)
    return pl.pallas_call(
        functools.partial(march_kernel, n_dev, RUN),
        out_shape=jax.ShapeDtypeStruct((STEPS, unk, exc), jnp.bfloat16),
        in_specs=[smem, smem, smem, hbm, hbm, hbm, hbm],
        out_specs=pl.BlockSpec(memory_space=pltpu.VMEM),
        scratch_shapes=[
            pltpu.VMEM((hist + 1,) + block, jnp.bfloat16),
            pltpu.VMEM((hist + 1,) + block, jnp.bfloat16),
            pltpu.VMEM((slots, band, unk, unk), jnp.bfloat16),
            pltpu.VMEM((unk, unk), jnp.bfloat16),
            pltpu.VMEM((STEPS, unk, exc), jnp.bfloat16),
            pltpu.VMEM((slots, halves) + block, jnp.float32),
            pltpu.VMEM((STEPS, halves, 11) + block, jnp.float32),
            pltpu.VMEM((2,) + block, jnp.bfloat16),
            pltpu.VMEM((STEPS, halves, KINDS) + block, jnp.float32),
            pltpu.VMEM((STEPS, halves, 3) + block, jnp.float32),
            pltpu.SemaphoreType.DMA((halves + 2,)),
            pltpu.SemaphoreType.DMA((unk // TILE,)),
            pltpu.SemaphoreType.DMA((STEPS, halves, KINDS, unk // TILE)),
            pltpu.SemaphoreType.DMA((STEPS, halves, KINDS, unk // TILE)),
        ],
        compiler_params=pltpu.CompilerParams(
            collective_id=0, has_side_effects=True, vmem_limit_bytes=62 * 2**20
        ),
        name="march",
    )(targets, delays, counts, couplings, history, diag_inverse, incident)


def solution(mesh):
    placed = (
        P(("group", "dev"), None, None, None, None),
        P(None, ("group", "dev"), None),
        P(("group", "dev"), None, None),
        P(None, ("group", "dev"), None),
        P(("group", "dev"), None),
        P(("group", "dev"), None),
        P(("group", "dev")),
    )
    return jax.shard_map(
        functools.partial(march, mesh.shape["dev"]),
        mesh=mesh,
        in_specs=placed,
        out_specs=P(None, ("group", "dev"), None),
        check_vma=False,
    )
```

```python
import functools

import jax
import jax.numpy as jnp
from jax import lax
from jax.experimental import pallas as pl
from jax.experimental.pallas import tpu as pltpu
from jax.sharding import PartitionSpec as P

BAND = 4
STEPS = 2
LANES = 128
TILE = 128
RUN = 4
MESH = pl.DeviceIdType.MESH

FAR, SUM, CHIP, JOIN, SKIP, MIDDLE, SIDE = 0, 2, 4, 5, 6, 7, 8
KINDS = 9


def march_kernel(
    n_dev,
    run,
    targets,
    delays,
    counts,
    couplings,
    history,
    diag,
    incident,
    out,
    past_0,
    past_1,
    mats,
    solve,
    shine,
    product,
    terms,
    current_box,
    box,
    chip_box,
    solved,
    result,
    load_sem,
    mat_sem,
    send_sem,
    recv_sem,
    out_sem,
):
    g = lax.axis_index("group")
    d = lax.axis_index("dev")
    slots = mats.shape[0]
    unk = mats.shape[2]
    halves = terms.shape[1]
    tiles = unk // TILE
    has_right, has_left = d < n_dev - 1, d > 0
    mate = g + 1 - 2 * (g % 2)
    crosses = (g == 1) | (g == 2)
    over = 3 - g
    x = d % run
    chip_code = 5 + 3 * (g % 2)
    over_code = 5 + 3 * (g // 2)
    even = x % 2 == 0
    at_start, at_end = x == 0, x == run - 1
    at_rim = at_start | at_end
    join_code = over_code + jnp.where(even, 2, 0)
    skip_code = over_code + jnp.where(even, 0, 2)
    join_group = jnp.where(at_rim, g, over)
    join_dev = d + jnp.where(at_start, 1, 0) - jnp.where(at_end, 1, 0)
    skip_dev = d - jnp.where(at_start, 1, 0) + jnp.where(at_end, 1, 0)
    skips = crosses & (skip_dev >= 0) & (skip_dev < n_dev)
    gathers = crosses & jnp.logical_not(at_rim)
    skip_into = jnp.where(at_rim, 2, jnp.where(even, 1, 3))
    side_into = jnp.where(even, 3, 1)
    near_side = jnp.where(at_start, 1, 0)
    skip_into = jnp.where(at_rim, 2, jnp.where(even, 1, 3))

    def tile_rows(r):
        return pl.ds(pl.multiple_of(r * TILE, TILE), TILE)

    past = (past_0, past_1)
    depth = past_0.shape[0] - 1

    def history_load(h):
        cols = pl.ds(h * LANES, LANES)
        return pltpu.make_async_copy(history.at[:, :, cols], past[h].at[pl.ds(1, depth)], load_sem.at[h])

    solve_load = pltpu.make_async_copy(diag.at[0], solve, load_sem.at[halves])
    shine_load = pltpu.make_async_copy(incident, shine, load_sem.at[halves + 1])

    def mat_load(r):
        rows = tile_rows(r)
        return pltpu.make_async_copy(couplings.at[0, :, :, rows, :], mats.at[:, :, rows, :], mat_sem.at[r])

    history_load(0).start()
    mat_load(0).start()
    for h in range(1, halves):
        history_load(h).start()

    @pl.loop(1, tiles)
    def _(r):
        mat_load(r).start()

    solve_load.start()
    shine_load.start()

    barrier = pltpu.get_barrier_semaphore()
    greeted = jnp.int32(1)
    pl.semaphore_signal(barrier, inc=1, device_id=(mate, d), device_id_type=MESH)
    for there, where in (
        (has_right, (g, d + 1)),
        (has_left, (g, d - 1)),
        (crosses, (over, d)),
        (skips & at_rim, (over, skip_dev)),
    ):

        @pl.when(there)
        def _():
            pl.semaphore_signal(barrier, inc=1, device_id=where, device_id_type=MESH)

        greeted = greeted + there.astype(jnp.int32)

    for held in past:
        held[0] = jnp.zeros_like(held[0])

    def copy_of(t, h, r, kind, side=0, leaving=False):
        code_is_chip = kind == CHIP
        inner = has_right & has_left
        aside = d + 1 - 2 * side
        beyond = aside + 1 - 2 * side
        inside = (aside >= 0) & (aside < n_dev)
        behind = d - 1 + 2 * side
        code, where, sends, hears = {
            FAR: (4 - 4 * side, (g, aside), (beyond >= 0) & (beyond < n_dev), inner),
            SUM: (3 - 2 * side, (g, aside), inside, (behind >= 0) & (behind < n_dev)),
            CHIP: (pl.ds(chip_code, 3), (mate, d), None, None),
            JOIN: (join_code, (join_group, join_dev), crosses, gathers),
            SIDE: (join_code, (join_group, join_dev), crosses, gathers),
            SKIP: (skip_code, (over, skip_dev), skips, skips),
            MIDDLE: (over_code + 1, (over, d), crosses, crosses),
        }[kind]
        rows = tile_rows(r)
        kind = jnp.where(at_rim, JOIN, SIDE) if leaving and kind == JOIN else kind + side
        target = chip_box.at[t, h, :, rows] if code_is_chip else box.at[t, h, kind, rows]
        copy = pltpu.make_async_remote_copy(
            src_ref=terms.at[t, h, code, rows],
            dst_ref=target,
            send_sem=send_sem.at[t, h, kind, r],
            recv_sem=recv_sem.at[t, h, kind, r],
            device_id=where,
            device_id_type=MESH,
        )
        return copy, sends, hears

    def when(there, do):
        if there is None:
            do()
        else:
            pl.when(there)(do)

    def send(t, h, r, kind, side=0):
        copy, sends, _ = copy_of(t, h, r, kind, side, True)
        when(sends, copy.start)

    def arrive(t, h, r, kind, side=0):
        copy, _, hears = copy_of(t, h, r, kind, side)
        when(hears, copy.wait_recv)

    live = [(jnp.int32(c) < counts[0]) for c in range(slots)]

    def weight(s, c):
        return jnp.where(live[c] & (targets[0, c] == s), 1.0, 0.0).astype(jnp.float32)

    weights = [[weight(s, c) for c in range(slots)] for s in range(11)]

    def gather_terms(t, h, r, codes):
        rows = tile_rows(r)
        parts = [product[c, h, rows, :] for c in range(slots)]
        for s in codes:
            total = parts[0] * weights[s][0]
            for c in range(1, slots):
                total = total + parts[c] * weights[s][c]
            terms[t, h, s, rows, :] = total

    def launch(t, h, r):
        gather_terms(t, h, r, (5, 6, 7))
        gather_terms(t, h, r, (8, 9, 10))
        for kind in (JOIN, SKIP, CHIP):
            send(t, h, r, kind)

        @pl.when(at_rim)
        def _():
            send(t, h, r, MIDDLE)

        gather_terms(t, h, r, (4, 0))
        for side in (0, 1):
            send(t, h, r, FAR, side)
        gather_terms(t, h, r, (3, 1, 2))

    def first_of(c):
        return jnp.maximum(delays[0, c], 1) - 1

    def products(shift, rows, over_halves):
        def taken(at):
            return jnp.concatenate([past[h][at] for h in over_halves], axis=1)

        @pl.loop(0, slots)
        def _(c):
            first = first_of(c) + shift
            total = jnp.dot(mats[c, 0, rows], taken(first), preferred_element_type=jnp.float32)
            for w in range(1, BAND):
                total = total + jnp.dot(mats[c, w, rows], taken(first + w), preferred_element_type=jnp.float32)
            for i, h in enumerate(over_halves):
                product[c, h, rows, :] = total[:, i * LANES : (i + 1) * LANES]

    def add(t, h, r, code, kind, there):
        rows = tile_rows(r)

        def do():
            terms[t, h, code, rows] = terms[t, h, code, rows] + box[t, h, kind, rows]

        when(there, do)

    def join(t, h, r):
        @pl.when(gathers)
        def _():
            arrive(t, h, r, JOIN)
            add(t, h, r, over_code + 1, JOIN, None)
            send(t, h, r, MIDDLE)

    def pass_on(t, h, r):
        rows = tile_rows(r)
        arrive(t, h, r, CHIP)
        arrive(t, h, r, SKIP)
        add(t, h, r, skip_into, SKIP, skips)
        arrive(t, h, r, SIDE)
        add(t, h, r, side_into, SIDE, gathers)
        for side in (near_side, 1 - near_side):
            code = 3 - 2 * side
            arrive(t, h, r, FAR, side)
            terms[t, h, code, rows] = terms[t, h, code, rows] + chip_box[t, h, code - 1, rows]
            add(t, h, r, code, FAR + side, has_right & has_left)
            send(t, h, r, SUM, side)

    def solve_step(t, h):
        cols = pl.ds(h * LANES, LANES)
        solved[...] = jnp.zeros_like(solved)

        @pl.loop(0, tiles)
        def _(r):
            rows = tile_rows(r)
            terms[t, h, 2, rows] = terms[t, h, 2, rows] + chip_box[t, h, 1, rows]
            for kind, side, there in ((MIDDLE, 0, crosses), (SUM, 0, has_left), (SUM, 1, has_right)):
                arrive(t, h, r, kind, side)
                add(t, h, r, 2, kind + side, there)
            right_side = (shine[t, rows, cols].astype(jnp.float32) - terms[t, h, 2, rows]).astype(jnp.bfloat16)
            solved[...] += jnp.dot(solve[:, rows], right_side, preferred_element_type=jnp.float32)

        current = solved[...].astype(jnp.bfloat16)
        result[t, h] = current
        out_copy(t, h).start()
        if t == 0:
            current_box[...] = current

    def out_copy(t, h):
        return pltpu.make_async_copy(result.at[t, h], out.at[t, :, pl.ds(h * LANES, LANES)], out_sem.at[t, h])

    fresh = [jnp.where(delays[0, c] == 1, 1.0, 0.0).astype(jnp.float32) for c in range(slots)]

    def refresh(h, rows):
        lead = mats[:, 0, rows, :].reshape(slots * TILE, unk)
        newest = jnp.dot(lead, current_box[...], preferred_element_type=jnp.float32)
        for c in range(slots):
            product[c, h, rows] = product[c, h, rows] + newest[c * TILE : (c + 1) * TILE] * fresh[c]

    every = list(range(halves))
    history_load(0).wait()
    mat_load(0).wait()
    products(1, tile_rows(0), every[:1])
    pl.semaphore_wait(barrier, greeted)
    launch(0, 0, 0)
    for h in every[1:]:
        history_load(h).wait()
        products(1, tile_rows(0), [h])
        launch(0, h, 0)

    @pl.loop(1, tiles)
    def _(r):
        mat_load(r).wait()
        products(1, tile_rows(r), every)
        for h in every:
            launch(0, h, r)
            join(0, h, r - 1)

    for h in every:
        join(0, h, tiles - 1)

    @pl.loop(0, tiles)
    def _(r):
        pass_on(0, 0, r)


    for h in every[1:]:

        @pl.loop(0, tiles)
        def _(r):
            pass_on(0, h, r)

    products(0, pl.ds(0, unk), every)
    solve_load.wait()
    shine_load.wait()
    for h in every:
        solve_step(0, h)

        @pl.loop(0, tiles)
        def _(r):
            refresh(h, tile_rows(r))
            launch(1, h, r)

            @pl.when(r > 0)
            def _():
                join(1, h, r - 1)

            if h:
                pass_on(1, h - 1, r)

        join(1, h, tiles - 1)

    @pl.loop(0, tiles)
    def _(r):
        pass_on(1, halves - 1, r)

    for h in every:
        solve_step(1, h)
    for t in range(STEPS):
        for h in range(halves):

            @pl.loop(0, tiles)
            def _(r):
                for kind, side in ((FAR, 0), (FAR, 1), (SUM, 0), (SUM, 1), (CHIP, 0), (JOIN, 0), (SKIP, 0), (MIDDLE, 0)):
                    copy, sends, _ = copy_of(t, h, r, kind, side, True)
                    when(sends, copy.wait_send)

            out_copy(t, h).wait()


def march(n_dev, couplings, history, diag_inverse, incident, targets, delays, counts):
    _, slots, band, unk, _ = couplings.shape
    hist, _, exc = history.shape
    halves = exc // LANES
    smem = pl.BlockSpec(memory_space=pltpu.SMEM)
    hbm = pl.BlockSpec(memory_space=pl.ANY)
    block = (unk, LANES)
    return pl.pallas_call(
        functools.partial(march_kernel, n_dev, RUN),
        out_shape=jax.ShapeDtypeStruct((STEPS, unk, exc), jnp.bfloat16),
        in_specs=[smem, smem, smem, hbm, hbm, hbm, hbm],
        out_specs=hbm,
        scratch_shapes=[
            pltpu.VMEM((hist + 1,) + block, jnp.bfloat16),
            pltpu.VMEM((hist + 1,) + block, jnp.bfloat16),
            pltpu.VMEM((slots, band, unk, unk), jnp.bfloat16),
            pltpu.VMEM((unk, unk), jnp.bfloat16),
            pltpu.VMEM((STEPS, unk, exc), jnp.bfloat16),
            pltpu.VMEM((slots, halves) + block, jnp.float32),
            pltpu.VMEM((STEPS, halves, 11) + block, jnp.float32),
            pltpu.VMEM(block, jnp.bfloat16),
            pltpu.VMEM((STEPS, halves, KINDS) + block, jnp.float32),
            pltpu.VMEM((STEPS, halves, 3) + block, jnp.float32),
            pltpu.VMEM(block, jnp.float32),
            pltpu.VMEM((STEPS, halves) + block, jnp.bfloat16),
            pltpu.SemaphoreType.DMA((halves + 2,)),
            pltpu.SemaphoreType.DMA((unk // TILE,)),
            pltpu.SemaphoreType.DMA((STEPS, halves, KINDS, unk // TILE)),
            pltpu.SemaphoreType.DMA((STEPS, halves, KINDS, unk // TILE)),
            pltpu.SemaphoreType.DMA((STEPS, halves)),
        ],
        compiler_params=pltpu.CompilerParams(
            collective_id=0, has_side_effects=True, vmem_limit_bytes=62 * 2**20
        ),
        name="march",
    )(targets, delays, counts, couplings, history, diag_inverse, incident)


def solution(mesh):
    placed = (
        P(("group", "dev"), None, None, None, None),
        P(None, ("group", "dev"), None),
        P(("group", "dev"), None, None),
        P(None, ("group", "dev"), None),
        P(("group", "dev"), None),
        P(("group", "dev"), None),
        P(("group", "dev")),
    )
    return jax.shard_map(
        functools.partial(march, mesh.shape["dev"]),
        mesh=mesh,
        in_specs=placed,
        out_specs=P(None, ("group", "dev"), None),
        check_vma=False,
    )
```

```python
import functools

import jax
import jax.numpy as jnp
from jax import lax
from jax.experimental import pallas as pl
from jax.experimental.pallas import tpu as pltpu
from jax.sharding import PartitionSpec as P

BAND = 4
STEPS = 2
LANES = 128
TILE = 128
RUN = 4
MESH = pl.DeviceIdType.MESH

FAR, SUM, CHIP, JOIN, SKIP, MIDDLE, SIDE = 0, 2, 4, 5, 6, 7, 8
KINDS = 9


def march_kernel(
    n_dev,
    run,
    table,
    couplings,
    history,
    diag,
    incident,
    out,
    past_0,
    past_1,
    mats,
    solve,
    shine,
    product,
    terms,
    current_box,
    box,
    chip_box,
    solved,
    result,
    load_sem,
    mat_sem,
    send_sem,
    recv_sem,
    out_sem,
):
    g = lax.axis_index("group")
    d = lax.axis_index("dev")
    slots = mats.shape[0]

    def target(c):
        return table[0, c]

    def delay(c):
        return table[0, slots + c]

    count = table[0, 2 * slots]
    unk = mats.shape[2]
    halves = terms.shape[1]
    tiles = unk // TILE
    has_right, has_left = d < n_dev - 1, d > 0
    mate = g + 1 - 2 * (g % 2)
    crosses = (g == 1) | (g == 2)
    over = 3 - g
    x = d % run
    chip_code = 5 + 3 * (g % 2)
    over_code = 5 + 3 * (g // 2)
    even = x % 2 == 0
    at_start, at_end = x == 0, x == run - 1
    at_rim = at_start | at_end
    join_code = over_code + jnp.where(even, 2, 0)
    skip_code = over_code + jnp.where(even, 0, 2)
    join_group = jnp.where(at_rim, g, over)
    join_dev = d + jnp.where(at_start, 1, 0) - jnp.where(at_end, 1, 0)
    skip_dev = d - jnp.where(at_start, 1, 0) + jnp.where(at_end, 1, 0)
    skips = crosses & (skip_dev >= 0) & (skip_dev < n_dev)
    gathers = crosses & jnp.logical_not(at_rim)
    skip_into = jnp.where(at_rim, 2, jnp.where(even, 1, 3))
    side_into = jnp.where(even, 3, 1)
    near_side = jnp.where(at_start, 1, 0)
    skip_into = jnp.where(at_rim, 2, jnp.where(even, 1, 3))

    def tile_rows(r):
        return pl.ds(pl.multiple_of(r * TILE, TILE), TILE)

    past = (past_0, past_1)
    depth = past_0.shape[0] - 1

    def history_load(h):
        cols = pl.ds(h * LANES, LANES)
        return pltpu.make_async_copy(history.at[:, :, cols], past[h].at[pl.ds(1, depth)], load_sem.at[h])

    solve_load = pltpu.make_async_copy(diag.at[0], solve, load_sem.at[halves])
    shine_load = pltpu.make_async_copy(incident, shine, load_sem.at[halves + 1])

    def mat_load(r):
        rows = tile_rows(r)
        return pltpu.make_async_copy(couplings.at[0, :, :, rows, :], mats.at[:, :, rows, :], mat_sem.at[r])

    history_load(0).start()
    mat_load(0).start()
    for h in range(1, halves):
        history_load(h).start()

    @pl.loop(1, tiles)
    def _(r):
        mat_load(r).start()

    solve_load.start()
    shine_load.start()

    barrier = pltpu.get_barrier_semaphore()
    greeted = jnp.int32(1)
    pl.semaphore_signal(barrier, inc=1, device_id=(mate, d), device_id_type=MESH)
    for there, where in (
        (has_right, (g, d + 1)),
        (has_left, (g, d - 1)),
        (crosses, (over, d)),
        (skips & at_rim, (over, skip_dev)),
    ):

        @pl.when(there)
        def _():
            pl.semaphore_signal(barrier, inc=1, device_id=where, device_id_type=MESH)

        greeted = greeted + there.astype(jnp.int32)

    for held in past:
        held[0] = jnp.zeros_like(held[0])

    def copy_of(t, h, r, kind, side=0, leaving=False):
        code_is_chip = kind == CHIP
        inner = has_right & has_left
        aside = d + 1 - 2 * side
        beyond = aside + 1 - 2 * side
        inside = (aside >= 0) & (aside < n_dev)
        behind = d - 1 + 2 * side
        code, where, sends, hears = {
            FAR: (4 - 4 * side, (g, aside), (beyond >= 0) & (beyond < n_dev), inner),
            SUM: (3 - 2 * side, (g, aside), inside, (behind >= 0) & (behind < n_dev)),
            CHIP: (pl.ds(chip_code, 3), (mate, d), None, None),
            JOIN: (join_code, (join_group, join_dev), crosses, gathers),
            SIDE: (join_code, (join_group, join_dev), crosses, gathers),
            SKIP: (skip_code, (over, skip_dev), skips, skips),
            MIDDLE: (over_code + 1, (over, d), crosses, crosses),
        }[kind]
        rows = tile_rows(r)
        kind = jnp.where(at_rim, JOIN, SIDE) if leaving and kind == JOIN else kind + side
        target = chip_box.at[t, h, :, rows] if code_is_chip else box.at[t, h, kind, rows]
        copy = pltpu.make_async_remote_copy(
            src_ref=terms.at[t, h, code, rows],
            dst_ref=target,
            send_sem=send_sem.at[t, h, kind, r],
            recv_sem=recv_sem.at[t, h, kind, r],
            device_id=where,
            device_id_type=MESH,
        )
        return copy, sends, hears

    def when(there, do):
        if there is None:
            do()
        else:
            pl.when(there)(do)

    def send(t, h, r, kind, side=0):
        copy, sends, _ = copy_of(t, h, r, kind, side, True)
        when(sends, copy.start)

    def arrive(t, h, r, kind, side=0):
        copy, _, hears = copy_of(t, h, r, kind, side)
        when(hears, copy.wait_recv)

    live = [(jnp.int32(c) < count) for c in range(slots)]

    def weight(s, c):
        return jnp.where(live[c] & (target(c) == s), 1.0, 0.0).astype(jnp.float32)

    weights = [[weight(s, c) for c in range(slots)] for s in range(11)]

    def gather_terms(t, h, r, codes):
        rows = tile_rows(r)
        parts = [product[c, h, rows, :] for c in range(slots)]
        for s in codes:
            total = parts[0] * weights[s][0]
            for c in range(1, slots):
                total = total + parts[c] * weights[s][c]
            terms[t, h, s, rows, :] = total

    def launch(t, h, r):
        gather_terms(t, h, r, (5, 6, 7))
        gather_terms(t, h, r, (8, 9, 10))
        for kind in (JOIN, SKIP, CHIP):
            send(t, h, r, kind)

        @pl.when(at_rim)
        def _():
            send(t, h, r, MIDDLE)

        gather_terms(t, h, r, (4, 0))
        for side in (0, 1):
            send(t, h, r, FAR, side)
        gather_terms(t, h, r, (3, 1, 2))

    def first_of(c):
        return jnp.maximum(delay(c), 1) - 1

    def products(shift, rows, over_halves):
        def taken(at):
            return jnp.concatenate([past[h][at] for h in over_halves], axis=1)

        @pl.loop(0, slots)
        def _(c):
            first = first_of(c) + shift
            total = jnp.dot(mats[c, 0, rows], taken(first), preferred_element_type=jnp.float32)
            for w in range(1, BAND):
                total = total + jnp.dot(mats[c, w, rows], taken(first + w), preferred_element_type=jnp.float32)
            for i, h in enumerate(over_halves):
                product[c, h, rows, :] = total[:, i * LANES : (i + 1) * LANES]

    def add(t, h, r, code, kind, there):
        rows = tile_rows(r)

        def do():
            terms[t, h, code, rows] = terms[t, h, code, rows] + box[t, h, kind, rows]

        when(there, do)

    def join(t, h, r):
        @pl.when(gathers)
        def _():
            arrive(t, h, r, JOIN)
            add(t, h, r, over_code + 1, JOIN, None)
            send(t, h, r, MIDDLE)

    def pass_on(t, h, r):
        rows = tile_rows(r)
        arrive(t, h, r, CHIP)
        arrive(t, h, r, SKIP)
        add(t, h, r, skip_into, SKIP, skips)
        arrive(t, h, r, SIDE)
        add(t, h, r, side_into, SIDE, gathers)
        for side in (near_side, 1 - near_side):
            code = 3 - 2 * side
            arrive(t, h, r, FAR, side)
            terms[t, h, code, rows] = terms[t, h, code, rows] + chip_box[t, h, code - 1, rows]
            add(t, h, r, code, FAR + side, has_right & has_left)
            send(t, h, r, SUM, side)

    def solve_step(t, h):
        cols = pl.ds(h * LANES, LANES)
        solved[...] = jnp.zeros_like(solved)

        @pl.loop(0, tiles)
        def _(r):
            rows = tile_rows(r)
            terms[t, h, 2, rows] = terms[t, h, 2, rows] + chip_box[t, h, 1, rows]
            for kind, side, there in ((MIDDLE, 0, crosses), (SUM, 0, has_left), (SUM, 1, has_right)):
                arrive(t, h, r, kind, side)
                add(t, h, r, 2, kind + side, there)
            right_side = (shine[t, rows, cols].astype(jnp.float32) - terms[t, h, 2, rows]).astype(jnp.bfloat16)
            solved[...] += jnp.dot(solve[:, rows], right_side, preferred_element_type=jnp.float32)

        current = solved[...].astype(jnp.bfloat16)
        result[t, h] = current
        out_copy(t, h).start()
        if t == 0:
            current_box[...] = current

    def out_copy(t, h):
        return pltpu.make_async_copy(result.at[t, h], out.at[t, :, pl.ds(h * LANES, LANES)], out_sem.at[t, h])

    fresh = [jnp.where(delay(c) == 1, 1.0, 0.0).astype(jnp.float32) for c in range(slots)]

    def refresh(h, rows):
        lead = mats[:, 0, rows, :].reshape(slots * TILE, unk)
        newest = jnp.dot(lead, current_box[...], preferred_element_type=jnp.float32)
        for c in range(slots):
            product[c, h, rows] = product[c, h, rows] + newest[c * TILE : (c + 1) * TILE] * fresh[c]

    every = list(range(halves))
    history_load(0).wait()
    mat_load(0).wait()
    products(1, tile_rows(0), every[:1])
    pl.semaphore_wait(barrier, greeted)
    launch(0, 0, 0)
    for h in every[1:]:
        history_load(h).wait()
        products(1, tile_rows(0), [h])
        launch(0, h, 0)

    @pl.loop(1, tiles)
    def _(r):
        mat_load(r).wait()
        products(1, tile_rows(r), every)
        for h in every:
            launch(0, h, r)
            join(0, h, r - 1)

    for h in every:
        join(0, h, tiles - 1)

    @pl.loop(0, tiles)
    def _(r):
        pass_on(0, 0, r)


    for h in every[1:]:

        @pl.loop(0, tiles)
        def _(r):
            pass_on(0, h, r)

    products(0, pl.ds(0, unk), every)
    solve_load.wait()
    shine_load.wait()
    for h in every:
        solve_step(0, h)

        @pl.loop(0, tiles)
        def _(r):
            refresh(h, tile_rows(r))
            launch(1, h, r)

        @pl.loop(0, tiles)
        def _(r):
            join(1, h, r)
            if h:
                pass_on(1, h - 1, r)


    @pl.loop(0, tiles)
    def _(r):
        pass_on(1, halves - 1, r)

    for h in every:
        solve_step(1, h)
    for t in range(STEPS):
        for h in range(halves):

            @pl.loop(0, tiles)
            def _(r):
                for kind, side in ((FAR, 0), (FAR, 1), (SUM, 0), (SUM, 1), (CHIP, 0), (JOIN, 0), (SKIP, 0), (MIDDLE, 0)):
                    copy, sends, _ = copy_of(t, h, r, kind, side, True)
                    when(sends, copy.wait_send)

            out_copy(t, h).wait()


def march(n_dev, couplings, history, diag_inverse, incident, targets, delays, counts):
    _, slots, band, unk, _ = couplings.shape
    hist, _, exc = history.shape
    halves = exc // LANES
    table = jnp.concatenate([targets, delays, counts[None]], axis=1)
    smem = pl.BlockSpec(memory_space=pltpu.SMEM)
    hbm = pl.BlockSpec(memory_space=pl.ANY)
    block = (unk, LANES)
    return pl.pallas_call(
        functools.partial(march_kernel, n_dev, RUN),
        out_shape=jax.ShapeDtypeStruct((STEPS, unk, exc), jnp.bfloat16),
        in_specs=[smem, hbm, hbm, hbm, hbm],
        out_specs=hbm,
        scratch_shapes=[
            pltpu.VMEM((hist + 1,) + block, jnp.bfloat16),
            pltpu.VMEM((hist + 1,) + block, jnp.bfloat16),
            pltpu.VMEM((slots, band, unk, unk), jnp.bfloat16),
            pltpu.VMEM((unk, unk), jnp.bfloat16),
            pltpu.VMEM((STEPS, unk, exc), jnp.bfloat16),
            pltpu.VMEM((slots, halves) + block, jnp.float32),
            pltpu.VMEM((STEPS, halves, 11) + block, jnp.float32),
            pltpu.VMEM(block, jnp.bfloat16),
            pltpu.VMEM((STEPS, halves, KINDS) + block, jnp.float32),
            pltpu.VMEM((STEPS, halves, 3) + block, jnp.float32),
            pltpu.VMEM(block, jnp.float32),
            pltpu.VMEM((STEPS, halves) + block, jnp.bfloat16),
            pltpu.SemaphoreType.DMA((halves + 2,)),
            pltpu.SemaphoreType.DMA((unk // TILE,)),
            pltpu.SemaphoreType.DMA((STEPS, halves, KINDS, unk // TILE)),
            pltpu.SemaphoreType.DMA((STEPS, halves, KINDS, unk // TILE)),
            pltpu.SemaphoreType.DMA((STEPS, halves)),
        ],
        compiler_params=pltpu.CompilerParams(
            collective_id=0, has_side_effects=True, vmem_limit_bytes=53 * 2**20 + 2**17
        ),
        name="march",
    )(table, couplings, history, diag_inverse, incident)


def solution(mesh):
    placed = (
        P(("group", "dev"), None, None, None, None),
        P(None, ("group", "dev"), None),
        P(("group", "dev"), None, None),
        P(None, ("group", "dev"), None),
        P(("group", "dev"), None),
        P(("group", "dev"), None),
        P(("group", "dev")),
    )
    return jax.shard_map(
        functools.partial(march, mesh.shape["dev"]),
        mesh=mesh,
        in_specs=placed,
        out_specs=P(None, ("group", "dev"), None),
        check_vma=False,
    )
```

```python
import functools

import jax
import jax.numpy as jnp
from jax import lax
from jax.experimental import pallas as pl
from jax.experimental.pallas import tpu as pltpu
from jax.sharding import PartitionSpec as P

BAND = 4
STEPS = 2
LANES = 128
TILE = 128
RUN = 4
MESH = pl.DeviceIdType.MESH

FAR, SUM, CHIP, JOIN, SKIP, MIDDLE, SIDE = 0, 2, 4, 5, 6, 7, 8
KINDS = 9


def march_kernel(
    n_dev,
    run,
    table,
    couplings,
    history,
    diag,
    incident,
    out,
    past_0,
    past_1,
    mats,
    solve,
    shine,
    product,
    terms,
    current_box,
    box,
    chip_box,
    solved,
    result,
    load_sem,
    mat_sem,
    send_sem,
    recv_sem,
    out_sem,
):
    g = lax.axis_index("group")
    d = lax.axis_index("dev")
    slots = mats.shape[0]

    def target(c):
        return table[0, c]

    def delay(c):
        return table[0, slots + c]

    count = table[0, 2 * slots]
    unk = mats.shape[2]
    halves = terms.shape[1]
    tiles = unk // TILE
    has_right, has_left = d < n_dev - 1, d > 0
    mate = g + 1 - 2 * (g % 2)
    crosses = (g == 1) | (g == 2)
    over = 3 - g
    x = d % run
    chip_code = 5 + 3 * (g % 2)
    over_code = 5 + 3 * (g // 2)
    even = x % 2 == 0
    at_start, at_end = x == 0, x == run - 1
    at_rim = at_start | at_end
    join_code = over_code + jnp.where(even, 2, 0)
    skip_code = over_code + jnp.where(even, 0, 2)
    join_group = jnp.where(at_rim, g, over)
    join_dev = d + jnp.where(at_start, 1, 0) - jnp.where(at_end, 1, 0)
    skip_dev = d - jnp.where(at_start, 1, 0) + jnp.where(at_end, 1, 0)
    skips = crosses & (skip_dev >= 0) & (skip_dev < n_dev)
    gathers = crosses & jnp.logical_not(at_rim)
    skip_into = jnp.where(even, 1, 3)
    side_into = jnp.where(even, 3, 1)
    near_side = jnp.where(at_start, 1, 0)

    def tile_rows(r):
        return pl.ds(pl.multiple_of(r * TILE, TILE), TILE)

    past = (past_0, past_1)
    depth = past_0.shape[0] - 1

    def history_load(h):
        cols = pl.ds(h * LANES, LANES)
        return pltpu.make_async_copy(history.at[:, :, cols], past[h].at[pl.ds(1, depth)], load_sem.at[h])

    solve_load = pltpu.make_async_copy(diag.at[0], solve, load_sem.at[halves])
    shine_load = pltpu.make_async_copy(incident, shine, load_sem.at[halves + 1])

    def mat_load(r):
        rows = tile_rows(r)
        return pltpu.make_async_copy(couplings.at[0, :, :, rows, :], mats.at[:, :, rows, :], mat_sem.at[r])

    history_load(0).start()
    mat_load(0).start()
    for h in range(1, halves):
        history_load(h).start()

    @pl.loop(1, tiles)
    def _(r):
        mat_load(r).start()

    solve_load.start()
    shine_load.start()

    barrier = pltpu.get_barrier_semaphore()
    greeted = jnp.int32(1)
    pl.semaphore_signal(barrier, inc=1, device_id=(mate, d), device_id_type=MESH)
    for there, where in (
        (has_right, (g, d + 1)),
        (has_left, (g, d - 1)),
        (crosses, (over, d)),
        (skips & at_rim, (over, skip_dev)),
    ):

        @pl.when(there)
        def _():
            pl.semaphore_signal(barrier, inc=1, device_id=where, device_id_type=MESH)

        greeted = greeted + there.astype(jnp.int32)

    for held in past:
        held[0] = jnp.zeros_like(held[0])

    def copy_of(t, h, r, kind, side=0, leaving=False):
        code_is_chip = kind == CHIP
        inner = has_right & has_left
        aside = d + 1 - 2 * side
        beyond = aside + 1 - 2 * side
        inside = (aside >= 0) & (aside < n_dev)
        behind = d - 1 + 2 * side
        code, where, sends, hears = {
            FAR: (4 - 4 * side, (g, aside), (beyond >= 0) & (beyond < n_dev), inner),
            SUM: (3 - 2 * side, (g, aside), inside, (behind >= 0) & (behind < n_dev)),
            CHIP: (pl.ds(chip_code, 3), (mate, d), None, None),
            JOIN: (join_code, (join_group, join_dev), crosses, gathers),
            SIDE: (join_code, (join_group, join_dev), crosses, gathers),
            SKIP: (skip_code, (over, skip_dev), skips, skips),
            MIDDLE: (over_code + 1, (over, d), crosses, crosses),
        }[kind]
        rows = tile_rows(r)
        kind = jnp.where(at_rim, JOIN, SIDE) if leaving and kind == JOIN else kind + side
        target = chip_box.at[t, h, :, rows] if code_is_chip else box.at[t, h, kind, rows]
        copy = pltpu.make_async_remote_copy(
            src_ref=terms.at[t, h, code, rows],
            dst_ref=target,
            send_sem=send_sem.at[t, h, kind, r],
            recv_sem=recv_sem.at[t, h, kind, r],
            device_id=where,
            device_id_type=MESH,
        )
        return copy, sends, hears

    def when(there, do):
        if there is None:
            do()
        else:
            pl.when(there)(do)

    def send(t, h, r, kind, side=0):
        copy, sends, _ = copy_of(t, h, r, kind, side, True)
        when(sends, copy.start)

    def arrive(t, h, r, kind, side=0):
        copy, _, hears = copy_of(t, h, r, kind, side)
        when(hears, copy.wait_recv)

    live = [(jnp.int32(c) < count) for c in range(slots)]

    def weight(s, c):
        return jnp.where(live[c] & (target(c) == s), 1.0, 0.0).astype(jnp.float32)

    weights = [[weight(s, c) for c in range(slots)] for s in range(11)]

    def gather_terms(t, h, r, codes):
        rows = tile_rows(r)
        parts = [product[c, h, rows, :] for c in range(slots)]
        for s in codes:
            total = parts[0] * weights[s][0]
            for c in range(1, slots):
                total = total + parts[c] * weights[s][c]
            terms[t, h, s, rows, :] = total

    def launch(t, h, r):
        gather_terms(t, h, r, (5, 6, 7))
        gather_terms(t, h, r, (8, 9, 10))
        for kind in (JOIN, SKIP, CHIP):
            send(t, h, r, kind)

        @pl.when(at_rim)
        def _():
            send(t, h, r, MIDDLE)

        gather_terms(t, h, r, (4, 0))
        for side in (0, 1):
            send(t, h, r, FAR, side)
        gather_terms(t, h, r, (3, 1, 2))

    def first_of(c):
        return jnp.maximum(delay(c), 1) - 1

    def products(shift, rows, over_halves):
        def taken(at):
            return jnp.concatenate([past[h][at] for h in over_halves], axis=1)

        @pl.loop(0, slots)
        def _(c):
            first = first_of(c) + shift
            total = jnp.dot(mats[c, 0, rows], taken(first), preferred_element_type=jnp.float32)
            for w in range(1, BAND):
                total = total + jnp.dot(mats[c, w, rows], taken(first + w), preferred_element_type=jnp.float32)
            for i, h in enumerate(over_halves):
                product[c, h, rows, :] = total[:, i * LANES : (i + 1) * LANES]

    def add(t, h, r, code, kind, there):
        rows = tile_rows(r)

        def do():
            terms[t, h, code, rows] = terms[t, h, code, rows] + box[t, h, kind, rows]

        when(there, do)

    def join(t, h, r):
        @pl.when(gathers)
        def _():
            arrive(t, h, r, JOIN)
            add(t, h, r, over_code + 1, JOIN, None)
            send(t, h, r, MIDDLE)

    def pass_on(t, h, r):
        rows = tile_rows(r)
        arrive(t, h, r, CHIP)

        @pl.when(gathers)
        def _():
            for kind, code in ((SKIP, skip_into), (SIDE, side_into)):
                arrive(t, h, r, kind)
                add(t, h, r, code, kind, None)

        for side in (near_side, 1 - near_side):
            code = 3 - 2 * side
            arrive(t, h, r, FAR, side)
            terms[t, h, code, rows] = terms[t, h, code, rows] + chip_box[t, h, code - 1, rows]
            add(t, h, r, code, FAR + side, has_right & has_left)
            send(t, h, r, SUM, side)

    def solve_step(t, h):
        cols = pl.ds(h * LANES, LANES)
        solved[...] = jnp.zeros_like(solved)

        @pl.loop(0, tiles)
        def _(r):
            rows = tile_rows(r)
            terms[t, h, 2, rows] = terms[t, h, 2, rows] + chip_box[t, h, 1, rows]
            for kind, side, there in ((SKIP, 0, skips & at_rim), (MIDDLE, 0, crosses), (SUM, 0, has_left), (SUM, 1, has_right)):

                @pl.when(there)
                def _():
                    arrive(t, h, r, kind, side)
                    add(t, h, r, 2, kind + side, None)

            right_side = (shine[t, rows, cols].astype(jnp.float32) - terms[t, h, 2, rows]).astype(jnp.bfloat16)
            solved[...] += jnp.dot(solve[:, rows], right_side, preferred_element_type=jnp.float32)

        current = solved[...].astype(jnp.bfloat16)
        result[t, h] = current
        out_copy(t, h).start()
        if t == 0:
            current_box[...] = current

    def drain(t, h, kinds):
        @pl.loop(0, tiles)
        def _(r):
            for kind, side in kinds:
                copy, sends, _ = copy_of(t, h, r, kind, side, True)
                when(sends, copy.wait_send)

    def out_copy(t, h):
        return pltpu.make_async_copy(result.at[t, h], out.at[t, :, pl.ds(h * LANES, LANES)], out_sem.at[t, h])

    fresh = [jnp.where(delay(c) == 1, 1.0, 0.0).astype(jnp.float32) for c in range(slots)]

    def refresh(h, rows):
        lead = mats[:, 0, rows, :].reshape(slots * TILE, unk)
        newest = jnp.dot(lead, current_box[...], preferred_element_type=jnp.float32)
        for c in range(slots):
            product[c, h, rows] = product[c, h, rows] + newest[c * TILE : (c + 1) * TILE] * fresh[c]

    every = list(range(halves))
    history_load(0).wait()
    mat_load(0).wait()
    products(1, tile_rows(0), every[:1])
    pl.semaphore_wait(barrier, greeted)
    launch(0, 0, 0)
    for h in every[1:]:
        history_load(h).wait()
        products(1, tile_rows(0), [h])
        launch(0, h, 0)

    @pl.loop(1, tiles)
    def _(r):
        mat_load(r).wait()
        products(1, tile_rows(r), every)
        for h in every:
            launch(0, h, r)
            join(0, h, r - 1)

    for h in every:
        join(0, h, tiles - 1)

    @pl.loop(0, tiles)
    def _(r):
        pass_on(0, 0, r)


    for h in every[1:]:

        @pl.loop(0, tiles)
        def _(r):
            pass_on(0, h, r)

    products(0, pl.ds(0, unk), every)
    solve_load.wait()
    shine_load.wait()
    for h in every:
        solve_step(0, h)

        @pl.loop(0, tiles)
        def _(r):
            refresh(h, tile_rows(r))
            launch(1, h, r)

        @pl.loop(0, tiles)
        def _(r):
            join(1, h, r)
            if h:
                pass_on(1, h - 1, r)


    @pl.loop(0, tiles)
    def _(r):
        pass_on(1, halves - 1, r)

    early = ((FAR, 0), (FAR, 1), (CHIP, 0), (JOIN, 0), (SKIP, 0))
    late = ((SUM, 0), (SUM, 1), (MIDDLE, 0))
    for h in every:
        drain(0, h, early + late)
    for h in every[:-1]:
        solve_step(1, h)
        drain(1, h, early + late)
    drain(1, every[-1], early)
    solve_step(1, every[-1])
    drain(1, every[-1], late)
    for t in range(STEPS):
        for h in every:
            out_copy(t, h).wait()


def march(n_dev, couplings, history, diag_inverse, incident, targets, delays, counts):
    _, slots, band, unk, _ = couplings.shape
    hist, _, exc = history.shape
    halves = exc // LANES
    table = jnp.concatenate([targets, delays, counts[None]], axis=1)
    smem = pl.BlockSpec(memory_space=pltpu.SMEM)
    hbm = pl.BlockSpec(memory_space=pl.ANY)
    block = (unk, LANES)
    return pl.pallas_call(
        functools.partial(march_kernel, n_dev, RUN),
        out_shape=jax.ShapeDtypeStruct((STEPS, unk, exc), jnp.bfloat16),
        in_specs=[smem, hbm, hbm, hbm, hbm],
        out_specs=hbm,
        scratch_shapes=[
            pltpu.VMEM((hist + 1,) + block, jnp.bfloat16),
            pltpu.VMEM((hist + 1,) + block, jnp.bfloat16),
            pltpu.VMEM((slots, band, unk, unk), jnp.bfloat16),
            pltpu.VMEM((unk, unk), jnp.bfloat16),
            pltpu.VMEM((STEPS, unk, exc), jnp.bfloat16),
            pltpu.VMEM((slots, halves) + block, jnp.float32),
            pltpu.VMEM((STEPS, halves, 11) + block, jnp.float32),
            pltpu.VMEM(block, jnp.bfloat16),
            pltpu.VMEM((STEPS, halves, KINDS) + block, jnp.float32),
            pltpu.VMEM((STEPS, halves, 3) + block, jnp.float32),
            pltpu.VMEM(block, jnp.float32),
            pltpu.VMEM((STEPS, halves) + block, jnp.bfloat16),
            pltpu.SemaphoreType.DMA((halves + 2,)),
            pltpu.SemaphoreType.DMA((unk // TILE,)),
            pltpu.SemaphoreType.DMA((STEPS, halves, KINDS, unk // TILE)),
            pltpu.SemaphoreType.DMA((STEPS, halves, KINDS, unk // TILE)),
            pltpu.SemaphoreType.DMA((STEPS, halves)),
        ],
        compiler_params=pltpu.CompilerParams(
            collective_id=0, has_side_effects=True, vmem_limit_bytes=53 * 2**20 + 2**17
        ),
        name="march",
    )(table, couplings, history, diag_inverse, incident)


def solution(mesh):
    placed = (
        P(("group", "dev"), None, None, None, None),
        P(None, ("group", "dev"), None),
        P(("group", "dev"), None, None),
        P(None, ("group", "dev"), None),
        P(("group", "dev"), None),
        P(("group", "dev"), None),
        P(("group", "dev")),
    )
    return jax.shard_map(
        functools.partial(march, mesh.shape["dev"]),
        mesh=mesh,
        in_specs=placed,
        out_specs=P(None, ("group", "dev"), None),
        check_vma=False,
    )
```
